32 devices in a mesh: seq: 4 (over x, core), fsdp: 8 (over z, y).
Axes of the slice: x: 2, y: 2, z: 4, core: 2. Of those that a mesh axis runs over, the one named last changes fastest.
Arguments:
- hidden: float32 [8, 512, 768], P('fsdp', 'seq'), may hold values from -6 to 6
- cotangent: float32 [8, 512, 768], P('fsdp', 'seq'), may hold values from -6 to 6
- segments: int32 [8, 512], P('fsdp'), may hold values from 0 to 2, never falling along the last dimension, each value on 1 to 256 neighbouring positions
- in_weight: bfloat16 [2, 768, 3352], P(None, 'fsdp'), may hold values from -0.21875 to 0.21875
- out_weight: bfloat16 [2, 1536, 768], P(None, 'fsdp'), may hold values from -0.15625 to 0.15625
- conv_weight: bfloat16 [2, 4, 1792], P(None, None, 'fsdp'), may hold values from -3 to 3
- conv_bias: bfloat16 [2, 1792], P(None, 'fsdp'), may hold values from -0.5 to 0.5
- norm_gain: bfloat16 [2, 768], P(None, 'fsdp'), may hold values from 0.099609375 to 1.8984375
- gate_gain: bfloat16 [2, 1536], P(None, 'fsdp'), may hold values from 0.099609375 to 1.8984375
- a_log: float32 [2, 24], replicated, may hold values from -3 to 2.5
- dt_bias: float32 [2, 24], replicated, may hold values from -5 to -1
- d_skip: float32 [2, 24], replicated, may hold values from 0.5 to 2
Outputs:
- hidden_out: float32 [8, 512, 768], P('fsdp', 'seq')
- input_grad: float32 [8, 512, 768], P('fsdp', 'seq')
- grad_in_weight: float32 [2, 768, 3352], P(None, 'fsdp')
- grad_out_weight: float32 [2, 1536, 768], P(None, 'fsdp')
- grad_conv_weight: float32 [2, 4, 1792], P(None, None, 'fsdp')
- grad_conv_bias: float32 [2, 1792], P(None, 'fsdp')
- grad_norm_gain: float32 [2, 768], P(None, 'fsdp')
- grad_gate_gain: float32 [2, 1536], P(None, 'fsdp')
- grad_a_log: float32 [2, 24], replicated
- grad_dt_bias: float32 [2, 24], replicated
- grad_d_skip: float32 [2, 24], replicated
The draws below stay inside these ranges and needn't reach their ends.
Inputs may be any that keep to these rules, and one draw needn't show every extreme that they name: `segments`: in each sequence the ids never fall and start at 0; each id covers 1 to 256 positions, one exactly 256.
All inputs are finite; a program needn't handle non-finite values.
Results may differ from the reference program's by a relative error of at most 0.015.
Values may be sent and summed in bfloat16 or wider, within the bound.
A program may use at most 192 MiB of HBM per device.

```python
import math
from functools import partial
import jax
import jax.numpy as jnp
import numpy as np
from jax import lax

D = 768
HEADS = 24
NSTATE = 128
KCONV = 4
SPAN = 256
LAYERS = 2
E = 1536
CONVDIM = 1792
PROJ = 3352
LEN = 512
SEQS = 8


def level_of(rng, extent, cuts, smallest, high):
    factor_of = 1.0
    for dim, shards_of in cuts:
        draws = jax.random.uniform(jax.random.fold_in(jax.random.fold_in(rng, 6), dim), (shards_of,), jnp.float32, smallest / len(cuts), high / len(cuts))
        factor_of = factor_of * jnp.repeat(jnp.exp(draws), extent[dim] // shards_of).reshape((-1,) + (1,) * (len(extent) - 1 - dim))
    return factor_of


def length_profile(amount, total, most, skew):
    loads = [(1 << 20) // math.isqrt(grade ** skew) + 1 for grade in range(2, amount + 1)]
    surplus, holding = total - most - (amount - 1), [1] * (amount - 1)
    while surplus > 0:
        movable = [i for i in range(amount - 1) if holding[i] < most]
        whole, left = sum([loads[i] for i in movable]), surplus
        for i in movable:
            extra = min(most - holding[i], max(1, left * loads[i] // whole), surplus)
            holding[i] = holding[i] + extra
            surplus = surplus - extra
    return np.array([most] + holding)


def ragged_sizes(stream_key, count, total, reach, slope):
    if count == 2:
        one = jax.random.randint(stream_key, (), max(1, total - reach), min(reach, total - 1) + 1)
        return jnp.stack([one, total - one])
    lengths = jnp.asarray(length_profile(count, total, reach, slope), jnp.int32)
    pairs = (count - 1) // 2
    donor, receiver = lengths[1:1 + 2 * pairs:2], lengths[2:2 + 2 * pairs:2]
    margin = jnp.minimum(donor - 1, reach - receiver)
    passed = jax.random.randint(jax.random.fold_in(stream_key, 1), (pairs,), 0, 1 << 20) % (margin + 1)
    lengths = lengths.at[1:1 + 2 * pairs:2].set(donor - passed).at[2:2 + 2 * pairs:2].set(receiver + passed)
    return lengths[jax.random.permutation(jax.random.fold_in(stream_key, 2), count)]


def scatter_about(rng, shape, deviation, reach, shards=(), kind=jnp.bfloat16):
    result = jax.random.normal(rng, shape, jnp.float32) * deviation
    if len(shards) > 0:
        result = level_of(rng, shape, shards, -0.22, 0.18) * result
    return jnp.clip(result, min=-reach, max=reach).astype(kind)


def setup_inputs(seed: int = 0) -> dict:
    streams_of = jax.random.split(jax.random.key(seed), 13)
    hidden = scatter_about(streams_of[0], (SEQS, LEN, D), 1.0, 6.0, ((0, 8), (1, 4)), jnp.float32)
    cotangent = scatter_about(streams_of[1], (SEQS, LEN, D), 1.0, 6.0, ((0, 8), (1, 4)), jnp.float32)
    segments = jax.vmap(lambda own: jnp.searchsorted(jnp.cumsum(ragged_sizes(own, 3, LEN, LEN // 2, 2)), jnp.arange(LEN), side="right"))(jax.random.split(streams_of[2], SEQS)).reshape((SEQS, LEN)).astype(jnp.int32)
    in_weight = scatter_about(streams_of[3], (LAYERS, D, PROJ), D ** -0.5, 0.21875, ((1, 8),))
    out_weight = scatter_about(streams_of[4], (LAYERS, E, D), E ** -0.5, 0.15625, ((1, 8),))
    conv_weight = scatter_about(streams_of[5], (LAYERS, KCONV, CONVDIM), KCONV ** -0.5, 3.0, ((2, 8),))
    conv_bias = jnp.clip(jax.random.uniform(streams_of[6], (LAYERS, CONVDIM), jnp.float32, -0.5, 0.5) * level_of(streams_of[6], (LAYERS, CONVDIM), ((1, 8),), -0.4, 0.0), -0.5, 0.5).astype(jnp.bfloat16)
    norm_gain = jnp.clip(1.0 + 0.18 * jax.random.normal(streams_of[7], (LAYERS, D), jnp.float32), 0.099609375, 1.8984375).astype(jnp.bfloat16)
    gate_gain = jnp.clip(1.0 + 0.18 * jax.random.normal(streams_of[8], (LAYERS, E), jnp.float32), 0.099609375, 1.8984375).astype(jnp.bfloat16)
    a_log = jnp.clip(jax.random.uniform(streams_of[9], (LAYERS, HEADS), jnp.float32, -3.0, 2.5), -3.0, 2.5)
    dt_bias = jnp.clip(jax.random.uniform(streams_of[10], (LAYERS, HEADS), jnp.float32, -5.0, -1.0), -5.0, -1.0)
    d_skip = jnp.clip(jax.random.uniform(streams_of[11], (LAYERS, HEADS), jnp.float32, 0.5, 2.0), 0.5, 2.0)
    return {"hidden": hidden, "cotangent": cotangent, "segments": segments, "in_weight": in_weight, "out_weight": out_weight, "conv_weight": conv_weight, "conv_bias": conv_bias, "norm_gain": norm_gain, "gate_gain": gate_gain, "a_log": a_log, "dt_bias": dt_bias, "d_skip": d_skip}


EPS = 1e-05
PRECISE = lax.Precision.HIGHEST

def rms_norm(values, gain_vec):
    return values * lax.rsqrt(lax.optimization_barrier(jnp.mean(values * values, axis=-1, keepdims=True)) + EPS) * gain_vec

def gate_part(y_val, z_val, gain_vec):
    return rms_norm(y_val * jax.nn.silu(z_val), gain_vec)

def rounded(values):
    return lax.optimization_barrier(values.astype(jnp.bfloat16)).astype(jnp.float32)

def conv_silu(joined, conv_w, conv_b, segment):
    tap_count = conv_w.shape[0]
    length = joined.shape[0]
    padded = jnp.pad(joined, ((tap_count - 1, 0), (0, 0)))
    seg_pad = jnp.concatenate([jnp.full((tap_count - 1,), -1, dtype=jnp.int32), segment.astype(jnp.int32)])
    summed = jnp.zeros_like(joined) + conv_b[None, :]
    for offset in range(tap_count):
        same_doc = (seg_pad[offset:offset + length] == segment.astype(jnp.int32))[:, None]
        summed = summed + jnp.where(same_doc, padded[offset:offset + length] * conv_w[offset][None, :], 0.0)
    return jax.nn.silu(summed)

def ssd_mixer(x_in, bc_in, dt_in, conv_w, conv_b, a_log_h, dt_bias_h, d_skip_h, segment):
    head_count = dt_in.shape[1]
    inner_width = x_in.shape[1]
    headdim = inner_width // head_count
    nstate = bc_in.shape[1] // 2
    length = x_in.shape[0]
    blocks = length // SPAN
    active = conv_silu(jnp.concatenate([x_in, bc_in], axis=1), conv_w, conv_b, segment)
    x_act = active[:, :inner_width]
    b_act = active[:, inner_width:inner_width + nstate]
    c_act = active[:, inner_width + nstate:]
    delta = jax.nn.softplus(dt_in + dt_bias_h[None, :])
    log_decay = -jnp.exp(a_log_h)[None, :] * delta
    x_scaled = x_act.reshape(length, head_count, headdim) * delta[:, :, None]
    pieces_all = (x_scaled.reshape(blocks, SPAN, head_count, headdim), b_act.reshape(blocks, SPAN, nstate), c_act.reshape(blocks, SPAN, nstate), log_decay.reshape(blocks, SPAN, head_count), segment.astype(jnp.int32).reshape(blocks, SPAN))
    causal = jnp.arange(SPAN)[:, None] >= jnp.arange(SPAN)[None, :]

    def one_block(carried, pieces):
        carry_state, last_seg = carried
        x_block, b_block, c_block, decay_block, seg_block = pieces
        cumulated = jnp.cumsum(decay_block, axis=0).T
        kept_mask = (causal & (seg_block[:, None] == seg_block[None, :]))[None]
        log_gap = cumulated[:, :, None] - cumulated[:, None, :]
        weights = jnp.where(kept_mask, jnp.exp(jnp.where(kept_mask, log_gap, 0.0)), 0.0)
        inner_prod = jnp.einsum('in,jn->ij', c_block, b_block, precision=PRECISE)
        scores = weights * inner_prod[None]
        intra = jnp.einsum('hij,jhp->ihp', scores, x_block, precision=PRECISE)
        carry_in = jnp.where((seg_block == last_seg)[None, :], jnp.exp(cumulated), 0.0)
        inter = jnp.einsum('in,hpn->ihp', c_block, carry_state, precision=PRECISE) * carry_in.T[:, :, None]
        end_seg = seg_block[SPAN - 1]
        end_log = cumulated[:, SPAN - 1]
        tail_decay = jnp.where((seg_block == end_seg)[None, :], jnp.exp(end_log[:, None] - cumulated), 0.0)
        keep_old = jnp.where(end_seg == last_seg, jnp.exp(end_log), 0.0)
        x_tail = x_block * tail_decay.T[:, :, None]
        new_state = carry_state * keep_old[:, None, None] + jnp.einsum('jhp,jn->hpn', x_tail, b_block, precision=PRECISE)
        return ((new_state, end_seg), intra + inter)
    start = (jnp.zeros((head_count, headdim, nstate), jnp.float32), jnp.array(-1, dtype=jnp.int32))
    discard, outputs = lax.scan(one_block, start, pieces_all)
    return outputs.reshape(length, inner_width) + x_act * jnp.repeat(d_skip_h, headdim)[None, :]

def reference(hidden, cotangent, segments, in_weight, out_weight, conv_weight, conv_bias, norm_gain, gate_gain, a_log, dt_bias, d_skip):

    def per_sequence(grads, items):
        hidden_seq, cot_seq, seg_row = items
        saved = []
        current = hidden_seq
        mixer_fn = partial(ssd_mixer, segment=seg_row)
        for layer_idx in range(LAYERS):
            gain_one = norm_gain[layer_idx].astype(jnp.float32)
            normed_in = rms_norm(current, gain_one).astype(jnp.bfloat16)
            projected = jnp.dot(normed_in, in_weight[layer_idx], preferred_element_type=jnp.float32)
            gate_z = projected[:, :E]
            primals = (rounded(projected[:, E:2 * E]), rounded(projected[:, 2 * E:2 * E + 2 * NSTATE]), rounded(projected[:, 2 * E + 2 * NSTATE:]), conv_weight[layer_idx].astype(jnp.float32), conv_bias[layer_idx].astype(jnp.float32), a_log[layer_idx], dt_bias[layer_idx], d_skip[layer_idx])
            y_val = rounded(mixer_fn(*primals))
            gate_one = gate_gain[layer_idx].astype(jnp.float32)
            gated = gate_part(y_val, gate_z, gate_one).astype(jnp.bfloat16)
            saved.append((current, normed_in, gate_z, y_val, primals, gated, gain_one, gate_one))
            current = current + jnp.dot(gated, out_weight[layer_idx], preferred_element_type=jnp.float32)
        grad_now = cot_seq
        grad_list = list(grads)
        for layer_idx in reversed(range(LAYERS)):
            prior, normed_in, gate_z, y_val, primals, gated, gain_one, gate_one = saved[layer_idx]
            grad_b = grad_now.astype(jnp.bfloat16)
            grad_out_w = jnp.dot(gated.T, grad_b, preferred_element_type=jnp.float32)
            d_gated = jnp.dot(grad_b, out_weight[layer_idx].T, preferred_element_type=jnp.float32)
            discard, gate_back = jax.vjp(gate_part, y_val, gate_z, gate_one)
            d_y, d_gate_z, grad_gate = gate_back(d_gated)
            discard, mixer_back = jax.vjp(mixer_fn, *primals)
            d_x, d_bc, d_dt, grad_cw, grad_cb, grad_alog, grad_dtb, grad_dsk = mixer_back(rounded(d_y))
            d_proj = jnp.concatenate([d_gate_z, d_x, d_bc, d_dt], axis=1).astype(jnp.bfloat16)
            grad_in_w = jnp.dot(normed_in.T, d_proj, preferred_element_type=jnp.float32)
            d_normed = jnp.dot(d_proj, in_weight[layer_idx].T, preferred_element_type=jnp.float32)
            discard, norm_back = jax.vjp(rms_norm, prior, gain_one)
            d_hidden, grad_norm = norm_back(d_normed)
            grad_now = grad_now + d_hidden
            terms = (grad_in_w, grad_out_w, grad_cw, grad_cb, grad_norm, grad_gate, grad_alog, grad_dtb, grad_dsk)
            grad_list = [accum.at[layer_idx].add(term) for accum, term in zip(grad_list, terms)]
        return (tuple(grad_list), (current, grad_now))
    start = (jnp.zeros((LAYERS, D, PROJ), jnp.float32), jnp.zeros((LAYERS, E, D), jnp.float32), jnp.zeros((LAYERS, KCONV, CONVDIM), jnp.float32), jnp.zeros((LAYERS, CONVDIM), jnp.float32), jnp.zeros((LAYERS, D), jnp.float32), jnp.zeros((LAYERS, E), jnp.float32), jnp.zeros((LAYERS, HEADS), jnp.float32), jnp.zeros((LAYERS, HEADS), jnp.float32), jnp.zeros((LAYERS, HEADS), jnp.float32))
    grads, results = lax.scan(per_sequence, start, (hidden, cotangent, segments))
    hidden_out, input_grad = results
    return (hidden_out, input_grad, grads[0], grads[1], grads[2], grads[3], grads[4], grads[5], grads[6], grads[7], grads[8])
```

```python
from functools import partial

import jax
import jax.numpy as jnp
from jax import lax
from jax.sharding import PartitionSpec as P

D = 768
HEADS = 24
HEADDIM = 64
NSTATE = 128
KCONV = 4
SPAN = 256
LAYERS = 2
E = 1536
CONVDIM = 1792


EPS = 1e-05
PRECISE = lax.Precision.HIGHEST
BF = jnp.bfloat16
F32 = jnp.float32


def rms_norm(values, gain_vec):
    return values * lax.rsqrt(jnp.mean(values * values, axis=-1, keepdims=True) + EPS) * gain_vec


def conv_silu(joined, conv_w, conv_b, segment):
    tap_count = conv_w.shape[0]
    length = joined.shape[0]
    padded = jnp.pad(joined, ((tap_count - 1, 0), (0, 0)))
    seg_pad = jnp.concatenate([jnp.full((tap_count - 1,), -1, dtype=jnp.int32), segment])
    summed = jnp.zeros_like(joined) + conv_b[None, :]
    for offset in range(tap_count):
        same_doc = (seg_pad[offset : offset + length] == segment)[:, None]
        summed = summed + jnp.where(
            same_doc, padded[offset : offset + length] * conv_w[offset][None, :], 0.0
        )
    return jax.nn.silu(summed)


def ssd_mixer(x_in, bc_in, dt_in, conv_w, conv_b, a_log_h, dt_bias_h, d_skip_h, segment):
    length, inner_width = x_in.shape
    head_count = dt_in.shape[0]
    headdim = inner_width // head_count
    nstate = bc_in.shape[1] // 2
    blocks = length // SPAN
    active = conv_silu(jnp.concatenate([x_in, bc_in], axis=1), conv_w, conv_b, segment)
    x_act = active[:, :inner_width].reshape(length, head_count, headdim).transpose(1, 0, 2)
    b_act = active[:, inner_width : inner_width + nstate]
    c_act = active[:, inner_width + nstate :]
    delta = jax.nn.softplus(dt_in + dt_bias_h[:, None])
    log_decay = -jnp.exp(a_log_h)[:, None] * delta
    x_scaled = x_act * delta[:, :, None]
    rows = jnp.arange(SPAN)[:, None]
    cols = jnp.arange(SPAN)[None, :]
    upper = (rows <= cols).astype(F32)
    state = None
    last_seg = None
    outs = []
    for block in range(blocks):
        span = slice(block * SPAN, (block + 1) * SPAN)
        x_block, b_block, c_block = x_scaled[:, span], b_act[span], c_act[span]
        seg_block = segment[span]
        cumulated = jnp.dot(log_decay[:, span], upper, precision=PRECISE)
        kept = ((rows >= cols) & (seg_block[:, None] == seg_block[None, :]))[None]
        log_gap = cumulated[:, :, None] - cumulated[:, None, :]
        weights = jnp.where(kept, jnp.exp(jnp.where(kept, log_gap, 0.0)), 0.0)
        inner_prod = jnp.einsum("in,jn->ij", c_block, b_block)
        out = jnp.einsum("hij,hjp->hip", weights * inner_prod[None], x_block)
        end_seg = seg_block[SPAN - 1]
        end_log = cumulated[:, SPAN - 1 :]
        if block > 0:
            carry_in = jnp.where((seg_block == last_seg)[None, :], jnp.exp(cumulated), 0.0)
            out = out + jnp.einsum("in,hpn->hip", c_block, state) * carry_in[:, :, None]
        if block < blocks - 1:
            tail_decay = jnp.where((seg_block == end_seg)[None, :], jnp.exp(end_log - cumulated), 0.0)
            added = jnp.einsum("hjp,jn->hpn", x_block * tail_decay[:, :, None], b_block)
            if block > 0:
                keep_old = jnp.where(end_seg == last_seg, jnp.exp(end_log), 0.0)
                added = added + state * keep_old[:, :, None]
            state = added
        last_seg = end_seg
        outs.append(out)
    total = jnp.concatenate(outs, axis=1) + x_act * d_skip_h[:, None, None]
    return total.transpose(1, 0, 2).reshape(length, inner_width)


def body(
    hidden,
    cotangent,
    segments,
    in_weight,
    out_weight,
    conv_weight,
    conv_bias,
    norm_gain,
    gate_gain,
    a_log,
    dt_bias,
    d_skip,
):
    current = hidden[0]
    seg_row = segments[0]
    seq_idx = lax.axis_index("seq")
    seq_count = lax.axis_size("seq")
    fsdp_count = lax.axis_size("fsdp")
    layers, taps, conv_part = conv_weight.shape
    width_part = norm_gain.shape[1]
    inner_part = gate_gain.shape[1]
    heads = a_log.shape[1]
    width = width_part * fsdp_count
    inner = inner_part * fsdp_count
    convdim = conv_part * fsdp_count
    bc_width = convdim - inner
    hl = heads // seq_count
    il = inner // seq_count
    bl = bc_width // seq_count
    dl = width // seq_count
    mixer_fn = partial(ssd_mixer, segment=seg_row)

    def swap(blocks):
        return lax.all_to_all(blocks, "fsdp", split_axis=0, concat_axis=0, tiled=True)

    def spread(arr):
        return swap(jnp.broadcast_to(arr[None], (fsdp_count,) + arr.shape))

    def owner_sum(full):
        blocks = swap(full.reshape((fsdp_count, full.shape[0] // fsdp_count) + full.shape[1:]))
        return jnp.sum(blocks.astype(F32), axis=0).astype(BF)

    def mine(arr, size, axis, base=0):
        return lax.dynamic_slice_in_dim(arr, base + seq_idx * size, size, axis)

    small = jnp.concatenate(
        [
            conv_weight.reshape(layers * taps, conv_part).reshape(-1),
            conv_bias.reshape(-1),
            norm_gain.reshape(-1),
            gate_gain.reshape(-1),
        ]
    )
    small_all = spread(small).astype(F32)

    def unpack(start, lead, part):
        piece = small_all[:, start : start + lead * part].reshape(fsdp_count, lead, part)
        return piece.transpose(1, 0, 2).reshape(lead, fsdp_count * part), start + lead * part

    conv_full, pos = unpack(0, layers * taps, conv_part)
    bias_full, pos = unpack(pos, layers, conv_part)
    norm_full, pos = unpack(pos, layers, width_part)
    gate_full, pos = unpack(pos, layers, inner_part)
    conv_full = conv_full.reshape(layers, taps, convdim)
    conv_loc = jnp.concatenate([mine(conv_full, il, 2), conv_full[:, :, inner:]], axis=2)
    bias_loc = jnp.concatenate([mine(bias_full, il, 1), bias_full[:, inner:]], axis=1)
    gate_loc = mine(gate_full, il, 1)
    alog_loc, dtb_loc, dsk_loc = mine(a_log, hl, 1), mine(dt_bias, hl, 1), mine(d_skip, hl, 1)
    dt_base = 2 * inner + bc_width

    in_loc, out_loc = [], []
    for l in range(layers):
        wl = in_weight[l]
        quarter = jnp.concatenate(
            [
                mine(wl, il, 1),
                mine(wl, il, 1, inner),
                wl[:, 2 * inner : dt_base],
                mine(wl, hl, 1, dt_base),
            ],
            axis=1,
        )
        in_loc.append(lax.all_gather(quarter, "fsdp", axis=0, tiled=True))
        cols = spread(mine(out_weight[l], dl, 1)).reshape(inner, dl)
        out_loc.append(lax.all_to_all(cols, "seq", split_axis=0, concat_axis=1, tiled=True))

    saved = []
    for l in range(layers):
        normed = rms_norm(current, norm_full[l]).astype(BF)
        normed_all = lax.all_gather(normed, "seq", axis=0, tiled=True)
        projected = jnp.dot(normed_all, in_loc[l], preferred_element_type=F32)
        gate_z = projected[:, :il]
        raw = projected[:, il:].astype(BF).astype(F32)
        primals = (
            raw[:, :il],
            raw[:, il : il + bc_width],
            raw[:, il + bc_width :].T,
            conv_loc[l],
            bias_loc[l],
            alog_loc[l],
            dtb_loc[l],
            dsk_loc[l],
        )
        y_full, mixer_back = jax.vjp(mixer_fn, *primals)
        y_val = y_full.astype(BF).astype(F32)
        prod = y_val * jax.nn.silu(gate_z)
        square = lax.psum(jnp.sum(prod * prod, axis=1), "seq")
        inv = lax.rsqrt(square / inner + EPS)
        scaled = (prod * gate_loc[l][None, :]).astype(BF)
        part = jnp.dot(scaled, out_loc[l], preferred_element_type=F32).astype(BF)
        rows_out = lax.psum_scatter(part, "seq", scatter_dimension=0, tiled=True).astype(F32)
        inv_own = mine(inv, current.shape[0], 0)
        delta_out = rows_out * inv_own[:, None]
        saved.append((current, normed_all, gate_z, y_val, prod, inv, scaled, delta_out, mixer_back))
        current = current + delta_out

    grad_now = cotangent[0]
    in_grads = [None] * layers
    out_grads = [None] * layers
    packed = [None] * layers
    for l in reversed(range(layers)):
        prior, normed_all, gate_z, y_val, prod, inv, scaled, delta_out, mixer_back = saved[l]
        grad_b = grad_now.astype(BF)
        dots = jnp.sum(grad_b.astype(F32) * delta_out, axis=1)
        grad_all = lax.all_gather(grad_b, "seq", axis=0, tiled=True)
        dots_all = lax.all_gather(dots, "seq", axis=0, tiled=True)
        d_gated = lax.dot_general(
            grad_all, out_loc[l], (((1,), (1,)), ((), ())), preferred_element_type=F32
        )
        scaled_in = d_gated * inv[:, None]
        grad_gate = jnp.sum(scaled_in * prod, axis=0)
        d_prod = scaled_in * gate_loc[l][None, :] - prod * (inv * inv * dots_all / inner)[:, None]
        sig = jax.nn.sigmoid(gate_z)
        silu_z = gate_z * sig
        d_y = (d_prod * silu_z).astype(BF).astype(F32)
        d_z = d_prod * y_val * (sig * (1.0 + gate_z * (1.0 - sig)))
        d_x, d_bc, d_dt, g_cw, g_cb, g_al, g_db, g_ds = mixer_back(d_y)
        d_bc_b = d_bc.astype(BF)
        d_zx = jnp.concatenate([d_z, d_x], axis=1).astype(BF)
        d_dt_b = d_dt.T.astype(BF)
        d_proj = jnp.concatenate([d_zx, d_bc_b, d_dt_b], axis=1)
        d_part = lax.dot_general(
            d_proj, in_loc[l], (((1,), (1,)), ((), ())), preferred_element_type=F32
        ).astype(BF)
        d_normed = lax.psum_scatter(d_part, "seq", scatter_dimension=0, tiled=True).astype(F32)
        discard, norm_back = jax.vjp(rms_norm, prior, norm_full[l])
        d_hidden, grad_norm = norm_back(d_normed)
        grad_now = grad_now + d_hidden

        d_bc_own = lax.all_to_all(
            d_bc_b.reshape(d_bc_b.shape[0], seq_count, bl).transpose(1, 0, 2),
            "seq",
            split_axis=0,
            concat_axis=0,
            tiled=True,
        )
        d_bc_own = jnp.sum(d_bc_own.astype(F32), axis=0).astype(BF)
        d_cols = jnp.concatenate([d_zx, d_bc_own, d_dt_b], axis=1)
        grad_in = lax.dot_general(
            normed_all, d_cols, (((0,), (0,)), ((), ())), preferred_element_type=F32
        ).astype(BF)
        in_grads[l] = owner_sum(grad_in)
        grad_scaled = (grad_all.astype(F32) * inv[:, None]).astype(BF)
        grad_out = lax.dot_general(
            scaled, grad_scaled, (((0,), (0,)), ((), ())), preferred_element_type=F32
        ).astype(BF)
        grad_out = lax.all_to_all(grad_out, "seq", split_axis=1, concat_axis=0, tiled=True)
        out_grads[l] = owner_sum(grad_out)

        five = jnp.concatenate([g_cw, g_cb[None]], axis=0)
        five_full = jnp.concatenate(
            [
                lax.dynamic_update_slice_in_dim(
                    jnp.zeros((taps + 1, inner), F32), five[:, :il], seq_idx * il, 1
                ),
                five[:, il:],
            ],
            axis=1,
        )
        gate_term = lax.dynamic_update_slice_in_dim(
            jnp.zeros((inner,), F32), grad_gate, seq_idx * il, 0
        )
        head_term = lax.dynamic_update_slice_in_dim(
            jnp.zeros((3, heads), F32), jnp.stack([g_al, g_db, g_ds]), seq_idx * hl, 1
        )
        packed[l] = jnp.concatenate(
            [
                five_full.reshape(taps + 1, fsdp_count, conv_part)
                .transpose(1, 0, 2)
                .reshape(fsdp_count, -1),
                grad_norm.reshape(fsdp_count, width_part),
                gate_term.reshape(fsdp_count, inner_part),
                jnp.broadcast_to(head_term.reshape(1, -1), (fsdp_count, 3 * heads)),
            ],
            axis=1,
        )

    sums = jnp.sum(swap(jnp.concatenate(packed, axis=1)), axis=0)
    sums = jnp.sum(lax.all_gather(sums, "seq", axis=0), axis=0).reshape(layers, -1)
    pos = (taps + 1) * conv_part
    five_own = sums[:, :pos].reshape(layers, taps + 1, conv_part)
    norm_own = sums[:, pos : pos + width_part]
    gate_own = sums[:, pos + width_part : pos + width_part + inner_part]
    head_sum = sums[:, pos + width_part + inner_part :].reshape(layers, 3, heads)

    in_out, out_out = [], []
    in_all = lax.all_gather(jnp.stack(in_grads), "seq", axis=0)
    out_all = lax.all_gather(jnp.stack(out_grads), "seq", axis=0)
    for l in range(layers):
        pieces = in_all[:, l]
        cuts = (0, il, 2 * il, 2 * il + bl, 2 * il + bl + hl)
        in_out.append(
            jnp.concatenate(
                [
                    pieces[s, :, cuts[k] : cuts[k + 1]]
                    for k in range(4)
                    for s in range(seq_count)
                ],
                axis=1,
            ).astype(F32)
        )
        halves = out_all[:, l]
        out_out.append(
            jnp.concatenate([halves[s] for s in range(seq_count)], axis=1).astype(F32)
        )
    return (
        current[None],
        grad_now[None],
        jnp.stack(in_out),
        jnp.stack(out_out),
        five_own[:, :taps],
        five_own[:, taps],
        norm_own,
        gate_own,
        head_sum[:, 0],
        head_sum[:, 1],
        head_sum[:, 2],
    )


def solution(mesh):
    placed = (
        P("fsdp", "seq", None),
        P("fsdp", "seq", None),
        P("fsdp", None),
        P(None, "fsdp", None),
        P(None, "fsdp", None),
        P(None, None, "fsdp"),
        P(None, "fsdp"),
        P(None, "fsdp"),
        P(None, "fsdp"),
        P(),
        P(),
        P(),
    )
    return jax.shard_map(
        body,
        mesh=mesh,
        in_specs=placed,
        out_specs=(
            P("fsdp", "seq", None),
            P("fsdp", "seq", None),
            P(None, "fsdp", None),
            P(None, "fsdp", None),
            P(None, None, "fsdp"),
            P(None, "fsdp"),
            P(None, "fsdp"),
            P(None, "fsdp"),
            P(),
            P(),
            P(),
        ),
        check_vma=False,
    )
```
